512 devices in a mesh: cells: 32 (over z, core), genes: 16 (over x, y).
Axes of the slice: x: 4, y: 4, z: 16, core: 2. Of those that a mesh axis runs over, the one named last changes fastest.
Arguments:
- sketch: bfloat16 [32768, 256], P('cells'), may hold values from -6 to 6
- tiles: bfloat16 [49152, 128, 128], P(('cells', 'genes')), may hold values from -0.0546875 to 0.0546875
- tile_rows: int32 [49152], P(('cells', 'genes')), may hold values from 0 to 7, as said below
- tile_cols: int32 [49152], P(('cells', 'genes')), may hold values from 0 to 15
- tile_counts: int32 [512], P(('cells', 'genes')), may hold values from 16 to 96, as said below
Outputs:
- projected: float32 [32768, 256], P(('cells', 'genes'))
The draws below stay inside these ranges and needn't reach their ends.
Inputs may be any that keep to these rules, and one draw needn't show every extreme that they name: Within one device's slots the pairs (tile_rows, tile_cols) are distinct. `tile_counts`: some device holds 96 tiles and the device half the cells axis away from it holds 16.
All inputs are finite; a program needn't handle non-finite values.
Results may differ from the reference program's by a relative error of at most 0.0021.
Values may be sent and summed in bfloat16 or wider, within the bound.
A program may use at most 128 MiB of HBM per device.

```python
import jax
import jax.numpy as jnp
from jax import lax

TILE = 128
RANK = 256
GENE_BLOCKS = 16
ROW_BLOCKS = 8
TMAX = 96
TMIN = 16
UNITS = 512
CELLS = 32768
N_CELLS = 32
N_GENES = 16


def place_slots(key):
    device_keys = jax.random.split(jax.random.fold_in(key, 11), UNITS)

    def one_device(device_key):
        return jax.random.permutation(device_key, ROW_BLOCKS * GENE_BLOCKS)[:TMAX]
    return jax.vmap(one_device)(device_keys).reshape(UNITS * TMAX).astype(jnp.int32)


def draw_tile_rows(key, part):
    return place_slots(key) // GENE_BLOCKS


def draw_tile_cols(key, part):
    return place_slots(key) % GENE_BLOCKS


def draw_tile_counts(key, part):
    first_draw = jax.random.randint(jax.random.fold_in(key, 1), (UNITS,), TMIN, TMAX + 1)
    second_draw = jax.random.randint(jax.random.fold_in(key, 2), (UNITS,), TMIN, TMAX + 1)
    third_draw = jax.random.randint(jax.random.fold_in(key, 3), (UNITS,), TMIN, TMAX + 1)
    counts = jnp.minimum(jnp.minimum(first_draw, second_draw), third_draw)
    counts = counts.at[0].set(TMAX).at[N_CELLS // 2 * N_GENES].set(TMIN)
    return counts.astype(jnp.int32)


def level_of(rng, shape, cuts, smallest, largest):
    loudness = 1.0
    for dim, blocks in cuts:
        heights = jax.random.uniform(jax.random.fold_in(jax.random.fold_in(rng, 6), dim), (blocks,), jnp.float32, smallest / len(cuts), largest / len(cuts))
        loudness = loudness * jnp.repeat(jnp.exp(heights), shape[dim] // blocks).reshape((-1,) + (1,) * (len(shape) - 1 - dim))
    return loudness


def bell_draw(key, extent, deviation, reach, shards=(), kind=jnp.bfloat16):
    array = deviation * jax.random.normal(key, extent, jnp.float32)
    if shards:
        array = array * level_of(key, extent, shards, -0.22, 0.18)
    return jnp.clip(array, -reach, reach).astype(kind)


def setup_inputs(seed: int = 0) -> dict:
    key_list = jax.random.split(jax.random.key(seed), 6)
    return {
        "sketch": bell_draw(key_list[0], (CELLS, RANK), 1.0, 6.0, ((0, 32),)),
        "tiles": bell_draw(key_list[1], (UNITS * TMAX, TILE, TILE), (TILE * TMAX) ** -0.5, 0.0546875, ((0, 512),)),
        "tile_rows": draw_tile_rows(jax.random.fold_in(key_list[5], 71), 0),
        "tile_cols": draw_tile_cols(jax.random.fold_in(key_list[5], 71), 0),
        "tile_counts": draw_tile_counts(jax.random.fold_in(key_list[5], 71), 0),
    }


def device_first(tile_set, row_ids, col_ids, count_one, sketch_rows):
    live_mask = (jnp.arange(TMAX, dtype=jnp.int32) < count_one).astype(jnp.float32)
    picked = sketch_rows[row_ids].astype(jnp.float32)
    contrib = jnp.einsum('ski,skr->sir', tile_set.astype(jnp.float32), picked)
    contrib = contrib * live_mask[:, None, None]
    return jnp.zeros((GENE_BLOCKS, TILE, RANK), jnp.float32).at[col_ids].add(contrib)


def device_second(tile_set, row_ids, col_ids, count_one, gene_rows):
    live_mask = (jnp.arange(TMAX, dtype=jnp.int32) < count_one).astype(jnp.float32)
    picked = gene_rows[col_ids].astype(jnp.float32)
    contrib = jnp.einsum('sik,skr->sir', tile_set.astype(jnp.float32), picked)
    contrib = contrib * live_mask[:, None, None]
    return jnp.zeros((ROW_BLOCKS, TILE, RANK), jnp.float32).at[row_ids].add(contrib)


def reference(sketch, tiles, tile_rows, tile_cols, tile_counts):
    tile_grid = tiles.reshape(N_CELLS, N_GENES, TMAX, TILE, TILE)
    row_grid = tile_rows.reshape(N_CELLS, N_GENES, TMAX)
    col_grid = tile_cols.reshape(N_CELLS, N_GENES, TMAX)
    count_grid = tile_counts.reshape(N_CELLS, N_GENES)
    sketch_grid = sketch.reshape(N_CELLS, ROW_BLOCKS, TILE, RANK)

    def gene_step(running, inputs):
        tile_set, row_ids, col_ids, count_row, sketch_rows = inputs
        partials = jax.vmap(device_first, in_axes=(0, 0, 0, 0, None))(tile_set, row_ids, col_ids, count_row, sketch_rows)
        return running + partials, None

    start_value = jnp.zeros((N_GENES, GENE_BLOCKS, TILE, RANK), jnp.float32)
    gene_side, _ = lax.scan(gene_step, start_value, (tile_grid, row_grid, col_grid, count_grid, sketch_grid))
    gene_cast = gene_side.astype(jnp.bfloat16)

    def cell_step(inputs):
        tile_set, row_ids, col_ids, count_row = inputs
        partials = jax.vmap(device_second)(tile_set, row_ids, col_ids, count_row, gene_cast)
        return jnp.sum(partials, axis=0)

    projected = lax.map(cell_step, (tile_grid, row_grid, col_grid, count_grid))
    return projected.reshape(N_CELLS * ROW_BLOCKS * TILE, RANK)
```

```python
import functools

import jax
import jax.numpy as jnp
from jax import lax
from jax.experimental import pallas as pl
from jax.experimental.pallas import tpu as pltpu
from jax.sharding import PartitionSpec as P

MESH = pl.DeviceIdType.MESH
TILE = 128
RS_PIECES = 4
AG_PIECES = 2
F32 = jnp.float32
BF16 = jnp.bfloat16


def mult(value, of):
    return pl.multiple_of(value, of)


def kernel(
    nz, side, sketch_hbm, tiles_hbm, rows_hbm, cols_hbm, count_hbm, out_ref,
    tiles, sketch, ids_r, ids_c, count, slot_v, slot_s, dense, qt, own, oth, prt,
    first, rr, gath, ysend, yown, yrecv,
    in_sem, prt_send, prt_recv, rs_send, rs_recv, ag_send, ag_recv, pg_send, pg_recv, y_send, y_recv,
):
    slots = tiles_hbm.shape[0]
    rank = sketch_hbm.shape[1]
    nh = nz // 2
    half = nz // 2 * TILE
    blocks = nz
    row_blocks = sketch_hbm.shape[0] // TILE
    pr = TILE // RS_PIECES
    pa = TILE // AG_PIECES

    cells = lax.axis_index("cells")
    genes = lax.axis_index("genes")
    z, core = cells // 2, cells % 2
    gx, gy = genes // side, genes % side
    right = ((z + 1) % nz * 2 + core, genes)
    left = ((z + nz - 1) % nz * 2 + core, genes)
    twin = (z * 2 + 1 - core, genes)
    ring = (right, left)

    def peer(ox, oy):
        return (cells, (gx + ox) % side * side + (gy + oy) % side)

    offsets = [(ox, oy) for ox in range(side) for oy in range(side)][1:]

    loads = [
        pltpu.make_async_copy(rows_hbm, ids_r, in_sem.at[0]),
        pltpu.make_async_copy(cols_hbm, ids_c, in_sem.at[1]),
        pltpu.make_async_copy(count_hbm, count, in_sem.at[2]),
        pltpu.make_async_copy(sketch_hbm, sketch, in_sem.at[3]),
        pltpu.make_async_copy(tiles_hbm, tiles.at[pl.ds(0, slots)], in_sem.at[4]),
    ]
    for load in loads:
        load.start()

    barrier = pltpu.get_barrier_semaphore()
    greeted = [right, left, twin] + [peer(ox, oy) for ox, oy in offsets]
    for who in greeted:
        pl.semaphore_signal(barrier, inc=1, device_id=who, device_id_type=MESH)

    tiles[slots] = jnp.zeros((TILE, TILE), BF16)
    for load in loads[:3]:
        load.wait()
    lane = lax.broadcasted_iota(jnp.int32, (1, slots), 1)
    key = jnp.where(lane < count[0], ids_r[...] * blocks + ids_c[...], -1)
    total = row_blocks * blocks
    where_j = lax.broadcasted_iota(jnp.int32, (total, slots), 0)
    which_s = lax.broadcasted_iota(jnp.int32, (total, slots), 1)
    hit = where_j == jnp.broadcast_to(key, (total, slots))
    picked = jnp.sum(jnp.where(hit, which_s - slots, 0), axis=1, keepdims=True) + slots
    diag = lax.broadcasted_iota(jnp.int32, (total, total), 0) == lax.broadcasted_iota(jnp.int32, (total, total), 1)
    row = jnp.sum(jnp.where(diag, jnp.broadcast_to(picked, (total, total)), 0), axis=0, keepdims=True)
    slot_v[...] = row
    to_smem = pltpu.make_async_copy(slot_v, slot_s, in_sem.at[5])
    to_smem.start()

    loads[3].wait()
    qt[...] = jnp.transpose(sketch[...])
    to_smem.wait()
    loads[4].wait()

    def place(r, carry):
        at = mult(r * TILE, TILE)
        for c in range(blocks):
            dense[pl.ds(at, TILE), c * TILE:(c + 1) * TILE] = tiles[jnp.clip(slot_s[0, r * blocks + c], 0, slots)]
        return carry
    lax.fori_loop(0, row_blocks, place, 0)

    pl.semaphore_wait(barrier, len(greeted))

    def product(offset, into):
        value = jnp.dot(qt[...], dense[:, pl.ds(mult(offset, 2 * TILE), 2 * TILE)], preferred_element_type=F32)
        into[0] = value[:, :TILE]
        into[1] = value[:, TILE:]

    pending = []
    swaps = []
    for q in range(nh // 2):
        product((1 - core) * half + q * 2 * TILE, oth.at[pl.ds(2 * q, 2)])
        swap = pltpu.make_async_remote_copy(
            oth.at[pl.ds(2 * q, 2)], prt.at[pl.ds(2 * q, 2)], prt_send.at[q], prt_recv.at[q],
            device_id=twin, device_id_type=MESH)
        swap.start()
        swaps.append(swap)
        pending.append(swap)
    for q in range(nh // 2):
        product(core * half + q * 2 * TILE, own.at[pl.ds(2 * q, 2)])
    for swap in swaps:
        swap.wait_recv()

    def mine(d, p):
        at = mult(d % 2 * TILE + p * pr, pr)
        return own[d // 2, pl.ds(at, pr), :] + prt[d // 2, pl.ds(at, pr), :]

    def hops(way, p):
        return nh - (way + p) % 2

    def toward(way, n):
        return (z + n) % nz if way == 0 else (z + nz - n) % nz

    def rs_copy(way, step, p, source):
        return pltpu.make_async_remote_copy(
            source, rr.at[way, step, pl.ds(p * pr, pr)], rs_send.at[way, step, p], rs_recv.at[way, step, p],
            device_id=ring[way], device_id_type=MESH)

    for p in range(RS_PIECES):
        for way in range(2):
            first[way, pl.ds(p * pr, pr)] = mine(toward(way, hops(way, p)), p)
            copy = rs_copy(way, 0, p, first.at[way, pl.ds(p * pr, pr)])
            copy.start()
            pending.append(copy)
    for s in range(1, nh + 1):
        for p in range(RS_PIECES):
            for way in range(2):
                n = hops(way, p)
                if s > n:
                    continue
                landed = rr.at[way, s - 1, pl.ds(p * pr, pr)]
                rs_copy(way, s - 1, p, landed).wait_recv()
                if s < n:
                    landed[...] = landed[...] + mine(toward(way, n - s), p)
                    copy = rs_copy(way, s, p, landed)
                    copy.start()
                    pending.append(copy)
    done = []
    for p in range(RS_PIECES):
        rows = pl.ds(p * pr, pr)
        done.append(mine(z, p) + rr[0, hops(0, p) - 1, rows] + rr[1, hops(1, p) - 1, rows])
    reduced = jnp.transpose(jnp.concatenate(done, axis=0)).astype(BF16)

    def place_of(who, d, p):
        return gath.at[pl.ds(mult(who * half + d // 2 * TILE + p * pa, pa), pa), pl.ds(mult(d % 2 * TILE, TILE), TILE)]

    def ag_copy(way, step, p, d):
        there = place_of(core, d, p)
        return pltpu.make_async_remote_copy(
            there, there, ag_send.at[way, step, p], ag_recv.at[way, step, p], device_id=ring[way], device_id_type=MESH)

    def pg_copy(index, p, who, d):
        there = place_of(who, d, p)
        return pltpu.make_async_remote_copy(
            there, there, pg_send.at[index, p], pg_recv.at[index, p], device_id=twin, device_id_type=MESH)

    arrivals = []
    for p in range(AG_PIECES):
        place_of(core, z, p)[...] = reduced[p * pa:(p + 1) * pa]
        for copy in [ag_copy(way, 0, p, z) for way in range(2)] + [pg_copy(0, p, core, z)]:
            copy.start()
            pending.append(copy)
        arrivals.append((0, p, z))
    for s in range(1, nh + 1):
        for p in range(AG_PIECES):
            for way in range(2):
                n = hops(way, p)
                if s > n:
                    continue
                d = toward(1 - way, s)
                ag_copy(way, s - 1, p, d).wait_recv()
                index = 1 + way * nh + s - 1
                onward = [pg_copy(index, p, core, d)]
                if s < n:
                    onward.insert(0, ag_copy(way, s, p, d))
                for copy in onward:
                    copy.start()
                    pending.append(copy)
                arrivals.append((index, p, d))
    for index, p, d in arrivals:
        pg_copy(index, p, 1 - core, d).wait_recv()

    keep = side * side
    part = dense.shape[0] // keep
    wide = part * side
    landings = []
    order = [side // 2] + [o for o in range(1, side) if o != side // 2] + [0]
    for ox in order:
        at = mult((gx + ox) % side * wide, wide)
        value = jnp.dot(dense[pl.ds(at, wide), :], gath[...], preferred_element_type=F32)
        if ox == 0:
            yown[...] = value
        ysend[ox] = value.astype(BF16)
        for oy in order:
            if ox == 0 and oy == 0:
                continue
            index = ox * side + oy
            copy = pltpu.make_async_remote_copy(
                ysend.at[ox, pl.ds(mult((gy + oy) % side * part, part), part)], yrecv.at[index],
                y_send.at[index], y_recv.at[index], device_id=peer(ox, oy), device_id_type=MESH)
            copy.start()
            pending.append(copy)
            landings.append((index, copy))
    result = yown[pl.ds(mult(gy * part, part), part), :]
    for index, copy in landings:
        copy.wait_recv()
        result = result + yrecv[index].astype(F32)
    out_ref[...] = result
    for copy in pending:
        copy.wait_send()


def solution(mesh):
    nz = mesh.shape["cells"] // 2
    side = {16: 4, 4: 2}[mesh.shape["genes"]]
    nh = nz // 2

    def local(sketch, tiles, tile_rows, tile_cols, tile_counts):
        slots = tiles.shape[0]
        rows, rank = sketch.shape
        part = rows // (side * side)
        dma = pltpu.SemaphoreType.DMA
        hbm = pl.BlockSpec(memory_space=pl.ANY)
        vmem = pltpu.VMEM
        return pl.pallas_call(
            functools.partial(kernel, nz, side),
            out_shape=jax.ShapeDtypeStruct((part, rank), F32),
            in_specs=[hbm] * 5,
            out_specs=pl.BlockSpec(memory_space=pltpu.VMEM),
            scratch_shapes=[
                vmem((slots + 1, TILE, TILE), BF16),
                vmem((rows, rank), BF16),
                vmem((1, slots), jnp.int32),
                vmem((1, slots), jnp.int32),
                pltpu.SMEM((1,), jnp.int32),
                vmem((1, rows // TILE * nz), jnp.int32),
                pltpu.SMEM((1, rows // TILE * nz), jnp.int32),
                vmem((rows, nz * TILE), BF16),
                vmem((rank, rows), BF16),
                vmem((nh, rank, TILE), F32),
                vmem((nh, rank, TILE), F32),
                vmem((nh, rank, TILE), F32),
                vmem((2, TILE, TILE), F32),
                vmem((2, nh, TILE, TILE), F32),
                vmem((nz * TILE, rank), BF16),
                vmem((side, part * side, rank), BF16),
                vmem((part * side, rank), F32),
                vmem((side * side, part, rank), BF16),
                dma((6,)),
                dma((nh // 2,)),
                dma((nh // 2,)),
                dma((2, nh, RS_PIECES)),
                dma((2, nh, RS_PIECES)),
                dma((2, nh, AG_PIECES)),
                dma((2, nh, AG_PIECES)),
                dma((1 + 2 * nh, AG_PIECES)),
                dma((1 + 2 * nh, AG_PIECES)),
                dma((side * side,)),
                dma((side * side,)),
            ],
            compiler_params=pltpu.CompilerParams(
                collective_id=0, has_side_effects=True, vmem_limit_bytes=67_000_000),
            name="power_pass",
        )(sketch, tiles, tile_rows.reshape(1, -1), tile_cols.reshape(1, -1), tile_counts)

    in_specs = (
        P("cells", None),
        P(("cells", "genes"), None, None),
        P(("cells", "genes")),
        P(("cells", "genes")),
        P(("cells", "genes")),
    )
    return jax.shard_map(
        local, mesh=mesh, in_specs=in_specs, out_specs=P(("cells", "genes"), None), check_vma=False)
```

```python
import functools

import jax
import jax.numpy as jnp
from jax import lax
from jax.experimental import pallas as pl
from jax.experimental.pallas import tpu as pltpu
from jax.sharding import PartitionSpec as P

MESH = pl.DeviceIdType.MESH
TILE = 128
PIECES = 2
CODED = True
PEAK = 32700.0
SCALE_ROWS = 16
ORDER = (2, 1, 3, 0)
UP = {1: 0, 2: 0, 3: 2, 4: 2, 5: 0, 6: 5, 7: 5, 8: 5}
F32 = jnp.float32
BF16 = jnp.bfloat16


def mult(value, of):
    return pl.multiple_of(value, of)


def kernel(
    nz, side, sketch_hbm, tiles_hbm, rows_hbm, cols_hbm, count_hbm, out_ref,
    tiles, sketch, ids_r, ids_c, count, slot_v, slot_s, dense, qt, own, oth, prt,
    first, rr, gath, ysend, yown, yrecv,
    in_sem, prt_send, prt_recv, rs_send, rs_recv, ag_send, ag_recv, pg_send, pg_recv, y_send, y_recv,
):
    slots = tiles_hbm.shape[0]
    rank = sketch_hbm.shape[1]
    nh = nz // 2
    half = nz // 2 * TILE
    blocks = nz
    row_blocks = sketch_hbm.shape[0] // TILE
    pr = TILE // PIECES

    cells = lax.axis_index("cells")
    genes = lax.axis_index("genes")
    z, core = cells // 2, cells % 2
    gx, gy = genes // side, genes % side
    twin = (z * 2 + 1 - core, genes)

    def along(way, n):
        return ((z + n) % nz if way == 0 else (z + nz - n) % nz)

    def ring(way, n):
        return (along(way, n) * 2 + core, genes)

    steps = sorted({j - UP[j] for j in range(1, nh + 1)})
    reach = sorted({n % nz for d in steps for n in (d, nz - d)})

    def peer(ox, oy):
        return (cells, (gx + ox) % side * side + (gy + oy) % side)

    offsets = [(ox, oy) for ox in range(side) for oy in range(side)][1:]

    barrier = pltpu.get_barrier_semaphore()
    greeted = [ring(0, n) for n in reach] + [twin] + [peer(ox, oy) for ox, oy in offsets]
    for who in greeted:
        pl.semaphore_signal(barrier, inc=1, device_id=who, device_id_type=MESH)

    loads = [
        pltpu.make_async_copy(rows_hbm, ids_r, in_sem.at[0]),
        pltpu.make_async_copy(cols_hbm, ids_c, in_sem.at[1]),
        pltpu.make_async_copy(count_hbm, count, in_sem.at[2]),
        pltpu.make_async_copy(sketch_hbm, sketch, in_sem.at[3]),
        pltpu.make_async_copy(tiles_hbm, tiles.at[pl.ds(0, slots)], in_sem.at[4]),
    ]
    for load in loads:
        load.start()

    tiles[slots] = jnp.zeros((TILE, TILE), BF16)
    for load in loads[:3]:
        load.wait()
    lane = lax.broadcasted_iota(jnp.int32, (1, slots), 1)
    key = jnp.where(lane < count[0], ids_r[...] * blocks + ids_c[...], -1)
    total = row_blocks * blocks
    where_j = lax.broadcasted_iota(jnp.int32, (total, slots), 0)
    which_s = lax.broadcasted_iota(jnp.int32, (total, slots), 1)
    hit = where_j == jnp.broadcast_to(key, (total, slots))
    picked = jnp.sum(jnp.where(hit, which_s - slots, 0), axis=1, keepdims=True) + slots
    diag = lax.broadcasted_iota(jnp.int32, (total, total), 0) == lax.broadcasted_iota(jnp.int32, (total, total), 1)
    row = jnp.sum(jnp.where(diag, jnp.broadcast_to(picked, (total, total)), 0), axis=0, keepdims=True)
    slot_v[...] = row
    to_smem = pltpu.make_async_copy(slot_v, slot_s, in_sem.at[5])
    to_smem.start()

    loads[3].wait()
    qt[...] = jnp.transpose(sketch[...])
    to_smem.wait()
    loads[4].wait()

    def place(r, carry):
        at = mult(r * TILE, TILE)
        for c in range(blocks):
            dense[pl.ds(at, TILE), c * TILE:(c + 1) * TILE] = tiles[jnp.clip(slot_s[0, r * blocks + c], 0, slots)]
        return carry
    lax.fori_loop(0, row_blocks, place, 0)

    pairs = nh // 2
    order_q = [(z // 4 + o) % pairs for o in ORDER if o < pairs]

    def product(offset, into):
        value = jnp.dot(qt[...], dense[:, pl.ds(mult(offset, 2 * TILE), 2 * TILE)], preferred_element_type=F32)
        into[0] = value[:, :TILE]
        into[1] = value[:, TILE:]

    for q in order_q:
        product((1 - core) * half + q * 2 * TILE, oth.at[pl.ds(2 * q, 2)])
    for q in order_q:
        product(core * half + q * 2 * TILE, own.at[pl.ds(2 * q, 2)])

    pl.semaphore_wait(barrier, len(greeted))
    pending = []
    swaps = []
    for k, q in enumerate(order_q):
        swap = pltpu.make_async_remote_copy(
            oth.at[pl.ds(2 * q, 2)], prt.at[pl.ds(2 * q, 2)], prt_send.at[k], prt_recv.at[k],
            device_id=twin, device_id_type=MESH)
        swap.start()
        swaps.append(swap)
        pending.append(swap)
    for swap in swaps:
        swap.wait_recv()

    def mine(d, p):
        at = mult(d % 2 * TILE + p * pr, pr)
        return own[d // 2, pl.ds(at, pr), :] + prt[d // 2, pl.ds(at, pr), :]

    def hops(way, p):
        return nh - (way + p) % 2

    def children(j, n):
        return [c for c in range(1, n + 1) if UP[c] == j]

    def encode(value, into):
        if not CODED:
            into[...] = value
            return
        peak = jnp.max(jnp.abs(value), axis=0, keepdims=True)
        power = jnp.floor(jnp.log2(jnp.maximum(peak, 1e-30))) + 1.0
        into[pl.ds(0, pr)] = jnp.round(value * (jnp.exp2(-power) * PEAK)).astype(jnp.int32).astype(jnp.int16)
        into[pl.ds(pr, SCALE_ROWS)] = jnp.broadcast_to(power, (SCALE_ROWS, TILE)).astype(jnp.int32).astype(jnp.int16)

    def decode(ref):
        if not CODED:
            return ref[...]
        power = ref[pl.ds(pr, SCALE_ROWS)].astype(jnp.int32).astype(F32)[0:1]
        return ref[pl.ds(0, pr)].astype(jnp.int32).astype(F32) * (jnp.exp2(power) * (1.0 / PEAK))

    def rs_copy(way, j, p):
        return pltpu.make_async_remote_copy(
            first.at[way, p, j - 1], rr.at[way, p, j - 1], rs_send.at[way, p, j - 1], rs_recv.at[way, p, j - 1],
            device_id=ring(way, j - UP[j]), device_id_type=MESH)

    def collect(way, j, p, total):
        for c in children(j, hops(way, p)):
            rs_copy(way, c, p).wait_recv()
            total = total + decode(rr.at[way, p, c - 1])
        return total

    deep = [j for j in range(nh, 0, -1) if UP[j]]
    heads = [j for j in range(nh, 0, -1) if not UP[j] and children(j, nh)]
    near = [j for j in range(nh, 0, -1) if not UP[j] and not children(j, nh)]
    for j in deep + heads + near:
        for p in range(PIECES):
            for way in range(2):
                if j > hops(way, p):
                    continue
                encode(collect(way, j, p, mine(along(way, j), p)), first.at[way, p, j - 1])
                copy = rs_copy(way, j, p)
                copy.start()
                pending.append(copy)
    done = []
    for p in range(PIECES):
        total = mine(z, p)
        for way in range(2):
            total = collect(way, 0, p, total)
        done.append(total)
    reduced = jnp.transpose(jnp.concatenate(done, axis=0)).astype(BF16)

    def place_of(who, d, p):
        return gath.at[pl.ds(mult(who * half + d // 2 * TILE + p * pr, pr), pr), pl.ds(mult(d % 2 * TILE, TILE), TILE)]

    def ag_copy(way, j, p, d):
        there = place_of(core, d, p)
        return pltpu.make_async_remote_copy(
            there, there, ag_send.at[way, p, j - 1], ag_recv.at[way, p, j - 1],
            device_id=ring(way, j - UP[j]), device_id_type=MESH)

    def pg_copy(index, p, who, d):
        there = place_of(who, d, p)
        return pltpu.make_async_remote_copy(
            there, there, pg_send.at[index, p], pg_recv.at[index, p], device_id=twin, device_id_type=MESH)

    def spread(way, j, p, d):
        for c in reversed(children(j, hops(way, p))):
            copy = ag_copy(way, c, p, d)
            copy.start()
            pending.append(copy)

    arrivals = []

    def share(index, p, d):
        copy = pg_copy(index, p, core, d)
        copy.start()
        pending.append(copy)
        arrivals.append((index, p, d))

    for p in range(PIECES):
        place_of(core, z, p)[...] = reduced[p * pr:(p + 1) * pr]
        for way in range(2):
            spread(way, 0, p, z)
    for p in range(PIECES):
        share(0, p, z)
    for j in heads[::-1] + near + deep[::-1]:
        for p in range(PIECES):
            for way in range(2):
                if j > hops(way, p):
                    continue
                d = along(1 - way, j)
                ag_copy(way, j, p, d).wait_recv()
                spread(way, j, p, d)
                share(1 + way * nh + j - 1, p, d)
    for index, p, d in arrivals:
        pg_copy(index, p, 1 - core, d).wait_recv()

    keep = side * side
    part = dense.shape[0] // keep
    wide = part * side
    landings = []
    order = [side // 2] + [o for o in range(1, side) if o != side // 2] + [0]
    for ox in order:
        at = mult((gx + ox) % side * wide, wide)
        value = jnp.dot(dense[pl.ds(at, wide), :], gath[...], preferred_element_type=F32)
        if ox == 0:
            yown[...] = value
        ysend[ox] = value.astype(BF16)
        for oy in order:
            if ox == 0 and oy == 0:
                continue
            index = ox * side + oy
            copy = pltpu.make_async_remote_copy(
                ysend.at[ox, pl.ds(mult((gy + oy) % side * part, part), part)], yrecv.at[index],
                y_send.at[index], y_recv.at[index], device_id=peer(ox, oy), device_id_type=MESH)
            copy.start()
            pending.append(copy)
            landings.append((index, copy))
    result = yown[pl.ds(mult(gy * part, part), part), :]
    for index, copy in landings:
        copy.wait_recv()
        result = result + yrecv[index].astype(F32)
    out_ref[...] = result
    for copy in pending:
        copy.wait_send()


def solution(mesh):
    nz = mesh.shape["cells"] // 2
    side = {16: 4, 4: 2}[mesh.shape["genes"]]
    nh = nz // 2

    def local(sketch, tiles, tile_rows, tile_cols, tile_counts):
        slots = tiles.shape[0]
        rows, rank = sketch.shape
        part = rows // (side * side)
        dma = pltpu.SemaphoreType.DMA
        kind = jnp.int16 if CODED else F32
        message = (2, PIECES, nh, TILE // PIECES + (SCALE_ROWS if CODED else 0), TILE)
        hbm = pl.BlockSpec(memory_space=pl.ANY)
        vmem = pltpu.VMEM
        return pl.pallas_call(
            functools.partial(kernel, nz, side),
            out_shape=jax.ShapeDtypeStruct((part, rank), F32),
            in_specs=[hbm] * 5,
            out_specs=pl.BlockSpec(memory_space=pltpu.VMEM),
            scratch_shapes=[
                vmem((slots + 1, TILE, TILE), BF16),
                vmem((rows, rank), BF16),
                vmem((1, slots), jnp.int32),
                vmem((1, slots), jnp.int32),
                pltpu.SMEM((1,), jnp.int32),
                vmem((1, rows // TILE * nz), jnp.int32),
                pltpu.SMEM((1, rows // TILE * nz), jnp.int32),
                vmem((rows, nz * TILE), BF16),
                vmem((rank, rows), BF16),
                vmem((nh, rank, TILE), F32),
                vmem((nh, rank, TILE), F32),
                vmem((nh, rank, TILE), F32),
                vmem(message, kind),
                vmem(message, kind),
                vmem((nz * TILE, rank), BF16),
                vmem((side, part * side, rank), BF16),
                vmem((part * side, rank), F32),
                vmem((side * side, part, rank), BF16),
                dma((6,)),
                dma((nh // 2,)),
                dma((nh // 2,)),
                dma((2, PIECES, nh)),
                dma((2, PIECES, nh)),
                dma((2, PIECES, nh)),
                dma((2, PIECES, nh)),
                dma((1 + 2 * nh, PIECES)),
                dma((1 + 2 * nh, PIECES)),
                dma((side * side,)),
                dma((side * side,)),
            ],
            compiler_params=pltpu.CompilerParams(
                collective_id=0, has_side_effects=True, vmem_limit_bytes=67_000_000),
            name="power_pass",
        )(sketch, tiles, tile_rows.reshape(1, -1), tile_cols.reshape(1, -1), tile_counts)

    in_specs = (
        P("cells", None),
        P(("cells", "genes"), None, None),
        P(("cells", "genes")),
        P(("cells", "genes")),
        P(("cells", "genes")),
    )
    return jax.shard_map(
        local, mesh=mesh, in_specs=in_specs, out_specs=P(("cells", "genes"), None), check_vma=False)
```

```python
import functools

import jax
import jax.numpy as jnp
from jax import lax
from jax.experimental import pallas as pl
from jax.experimental.pallas import tpu as pltpu
from jax.sharding import PartitionSpec as P

MESH = pl.DeviceIdType.MESH
TILE = 128
PIECES = 2
CODED = True
PEAK = 32700.0
SCALE_ROWS = 16
ORDER = (2, 1, 3, 0)
UP = {1: 0, 2: 0, 3: 2, 4: 2, 5: 0, 6: 5, 7: 5, 8: 5}
F32 = jnp.float32
BF16 = jnp.bfloat16


def mult(value, of):
    return pl.multiple_of(value, of)


def kernel(
    nz, side, sketch_hbm, tiles_hbm, rows_hbm, cols_hbm, count_hbm, out_ref,
    tiles, sketch, ids_r, ids_c, count, slot_v, slot_s, dense, qt, own, oth, prt,
    first, rr, gath, ysend, yown, yrecv,
    in_sem, prt_send, prt_recv, rs_send, rs_recv, ag_send, ag_recv, pg_send, pg_recv, y_send, y_recv, hint,
):
    slots = tiles_hbm.shape[0]
    rank = sketch_hbm.shape[1]
    nh = nz // 2
    half = nz // 2 * TILE
    blocks = nz
    row_blocks = sketch_hbm.shape[0] // TILE
    pr = TILE // PIECES

    cells = lax.axis_index("cells")
    genes = lax.axis_index("genes")
    z, core = cells // 2, cells % 2
    gx, gy = genes // side, genes % side
    twin = (z * 2 + 1 - core, genes)

    def along(way, n):
        return ((z + n) % nz if way == 0 else (z + nz - n) % nz)

    def ring(way, n):
        return (along(way, n) * 2 + core, genes)

    steps = sorted({j - UP[j] for j in range(1, nh + 1)} & {1, 2, 3})
    reach = sorted({n % nz for d in steps for n in (d, nz - d)})

    def peer(ox, oy):
        return (cells, (gx + ox) % side * side + (gy + oy) % side)

    offsets = [(ox, oy) for ox in range(side) for oy in range(side)][1:]
    close = [(ox, oy) for ox, oy in offsets if min(ox, side - ox) + min(oy, side - oy) <= 2]
    hints = [(1, 0), (side - 1, 0), (1, 1)] if len(close) < len(offsets) else []

    barrier = pltpu.get_barrier_semaphore()
    greeted = [ring(0, n) for n in reach] + [twin] + [peer(ox, oy) for ox, oy in close]
    for who in greeted:
        pl.semaphore_signal(barrier, inc=1, device_id=who, device_id_type=MESH)

    loads = [
        pltpu.make_async_copy(rows_hbm, ids_r, in_sem.at[0]),
        pltpu.make_async_copy(cols_hbm, ids_c, in_sem.at[1]),
        pltpu.make_async_copy(count_hbm, count, in_sem.at[2]),
        pltpu.make_async_copy(sketch_hbm, sketch, in_sem.at[3]),
        pltpu.make_async_copy(tiles_hbm, tiles.at[pl.ds(0, slots)], in_sem.at[4]),
    ]
    for load in loads:
        load.start()

    tiles[slots] = jnp.zeros((TILE, TILE), BF16)
    for load in loads[:3]:
        load.wait()
    lane = lax.broadcasted_iota(jnp.int32, (1, slots), 1)
    key = jnp.where(lane < count[0], ids_r[...] * blocks + ids_c[...], -1)
    total = row_blocks * blocks
    where_j = lax.broadcasted_iota(jnp.int32, (total, slots), 0)
    which_s = lax.broadcasted_iota(jnp.int32, (total, slots), 1)
    hit = where_j == jnp.broadcast_to(key, (total, slots))
    picked = jnp.sum(jnp.where(hit, which_s - slots, 0), axis=1, keepdims=True) + slots
    diag = lax.broadcasted_iota(jnp.int32, (total, total), 0) == lax.broadcasted_iota(jnp.int32, (total, total), 1)
    row = jnp.sum(jnp.where(diag, jnp.broadcast_to(picked, (total, total)), 0), axis=0, keepdims=True)
    slot_v[...] = row
    to_smem = pltpu.make_async_copy(slot_v, slot_s, in_sem.at[5])
    to_smem.start()

    loads[3].wait()
    qt[...] = jnp.transpose(sketch[...])
    to_smem.wait()
    loads[4].wait()

    def place(r, carry):
        at = mult(r * TILE, TILE)
        for c in range(blocks):
            dense[pl.ds(at, TILE), c * TILE:(c + 1) * TILE] = tiles[jnp.clip(slot_s[0, r * blocks + c], 0, slots)]
        return carry
    lax.fori_loop(0, row_blocks, place, 0)

    pairs = nh // 2
    order_q = [(z // 4 + o) % pairs for o in ORDER if o < pairs]

    def product(offset, into):
        value = jnp.dot(qt[...], dense[:, pl.ds(mult(offset, 2 * TILE), 2 * TILE)], preferred_element_type=F32)
        into[0] = value[:, :TILE]
        into[1] = value[:, TILE:]

    for q in order_q:
        product((1 - core) * half + q * 2 * TILE, oth.at[pl.ds(2 * q, 2)])
    for q in order_q:
        product(core * half + q * 2 * TILE, own.at[pl.ds(2 * q, 2)])

    pl.semaphore_wait(barrier, len(greeted))
    for k, (ox, oy) in enumerate(hints):
        pl.semaphore_signal(hint.at[k], inc=1, device_id=peer(side - ox, side - oy), device_id_type=MESH)
    pending = []
    swaps = []
    for k, q in enumerate(order_q):
        swap = pltpu.make_async_remote_copy(
            oth.at[pl.ds(2 * q, 2)], prt.at[pl.ds(2 * q, 2)], prt_send.at[k], prt_recv.at[k],
            device_id=twin, device_id_type=MESH)
        swap.start()
        swaps.append(swap)
        pending.append(swap)
    def mine(d, p):
        at = mult(p * TILE + d % 2 * pr, pr)
        return own[d // 2, pl.ds(at, pr), :] + prt[d // 2, pl.ds(at, pr), :]

    def hops(way, p):
        return nh - (way + p) % 2

    def children(j, n):
        return [c for c in range(1, n + 1) if UP[c] == j]

    def encode(value, into):
        if not CODED:
            into[...] = value
            return
        peak = jnp.max(jnp.abs(value), axis=0, keepdims=True)
        power = jnp.floor(jnp.log2(jnp.maximum(peak, 1e-30))) + 1.0
        into[pl.ds(0, pr)] = jnp.round(value * (jnp.exp2(-power) * PEAK)).astype(jnp.int32).astype(jnp.int16)
        into[pl.ds(pr, SCALE_ROWS)] = jnp.broadcast_to(power, (SCALE_ROWS, TILE)).astype(jnp.int32).astype(jnp.int16)

    def decode(ref):
        if not CODED:
            return ref[...]
        power = ref[pl.ds(pr, SCALE_ROWS)].astype(jnp.int32).astype(F32)[0:1]
        return ref[pl.ds(0, pr)].astype(jnp.int32).astype(F32) * (jnp.exp2(power) * (1.0 / PEAK))

    def rs_copy(way, j, p):
        return pltpu.make_async_remote_copy(
            first.at[way, p, j - 1], rr.at[way, p, j - 1], rs_send.at[way, p, j - 1], rs_recv.at[way, p, j - 1],
            device_id=ring(way, j - UP[j]), device_id_type=MESH)

    def collect(way, j, p, total):
        for c in children(j, hops(way, p)):
            rs_copy(way, c, p).wait_recv()
            total = total + decode(rr.at[way, p, c - 1])
        return total

    deep = [j for j in range(nh, 0, -1) if UP[j]]
    heads = [j for j in range(nh, 0, -1) if not UP[j] and children(j, nh)]
    near = [j for j in range(nh, 0, -1) if not UP[j] and not children(j, nh)]
    ready = {deep[0]: swaps[:1], deep[1]: swaps[1:3], deep[-1]: swaps[3:]} if len(swaps) == 4 else {nh: swaps}
    for j in deep + heads + near:
        for swap in ready.get(j, ()):
            swap.wait_recv()
        for p in range(PIECES):
            ways = [way for way in range(2) if j <= hops(way, p)]
            for way in ways:
                encode(collect(way, j, p, mine(along(way, j), p)), first.at[way, p, j - 1])
            for way in ways:
                copy = rs_copy(way, j, p)
                copy.start()
                pending.append(copy)

    def place_of(who, d, p):
        return gath.at[pl.ds(mult(p * TILE + d % 2 * pr, pr), pr), pl.ds(mult(who * half + d // 2 * TILE, TILE), TILE)]

    def ag_copy(way, j, p, d):
        there = place_of(core, d, p)
        return pltpu.make_async_remote_copy(
            there, there, ag_send.at[way, p, j - 1], ag_recv.at[way, p, j - 1],
            device_id=ring(way, j - UP[j]), device_id_type=MESH)

    def pg_copy(index, p, who, d):
        there = place_of(who, d, p)
        return pltpu.make_async_remote_copy(
            there, there, pg_send.at[index, p], pg_recv.at[index, p], device_id=twin, device_id_type=MESH)

    def spread(way, j, p, d):
        for c in reversed(children(j, hops(way, p))):
            copy = ag_copy(way, c, p, d)
            copy.start()
            pending.append(copy)

    def share(index, p, d):
        copy = pg_copy(index, p, core, d)
        copy.start()
        pending.append(copy)

    def receive(j, p):
        for way in range(2):
            if j > hops(way, p):
                continue
            d = along(1 - way, j)
            ag_copy(way, j, p, d).wait_recv()
            spread(way, j, p, d)
            share(1 + way * nh + j - 1, p, d)

    def receive_shared(p):
        pg_copy(0, p, 1 - core, z).wait_recv()
        for j in range(1, nh + 1):
            for way in range(2):
                if j <= hops(way, p):
                    pg_copy(1 + way * nh + j - 1, p, 1 - core, along(1 - way, j)).wait_recv()

    for p in range(PIECES):
        total = mine(z, p)
        for way in range(2):
            total = collect(way, 0, p, total)
        place_of(core, z, p)[...] = total.astype(BF16)
        for way in range(2):
            spread(way, 0, p, z)
        share(0, p, z)

    part = dense.shape[0] // (side * side)
    wide = part * side
    landings = [[], []]
    order = [side // 2] + [o for o in range(1, side) if o != side // 2] + [0]

    def project(ox, p):
        at = mult((gx + ox) % side * wide, wide)
        value = lax.dot_general(
            dense[pl.ds(at, wide), :], gath[p * TILE:(p + 1) * TILE, :], (((1,), (1,)), ((), ())),
            preferred_element_type=F32)
        if ox == 0:
            yown[p] = value
        ysend[p, ox] = value.astype(BF16)
        for oy in order:
            if ox == 0 and oy == 0:
                continue
            index = ox * side + oy
            copy = pltpu.make_async_remote_copy(
                ysend.at[p, ox, pl.ds(mult((gy + oy) % side * part, part), part)], yrecv.at[p, index],
                y_send.at[p, index], y_recv.at[p, index], device_id=peer(ox, oy), device_id_type=MESH)
            copy.start()
            pending.append(copy)
            landings[p].append((index, copy))

    for k in range(len(hints)):
        pl.semaphore_wait(hint.at[k], 1)
    for j in heads[::-1]:
        for p in range(PIECES):
            receive(j, p)
    for j in near + deep[::-1]:
        receive(j, 0)
    receive_shared(0)
    later = near + deep[::-1]
    share_of = -(-len(later) // side)
    for k, ox in enumerate(order):
        project(ox, 0)
        for j in later[k * share_of:(k + 1) * share_of]:
            receive(j, 1)
    receive_shared(1)
    for ox in order:
        project(ox, 1)
    for p in range(PIECES):
        result = yown[p, pl.ds(mult(gy * part, part), part), :]
        for index, copy in landings[p]:
            copy.wait_recv()
            result = result + yrecv[p, index].astype(F32)
        out_ref[:, p * TILE:(p + 1) * TILE] = result
    for copy in pending:
        copy.wait_send()


def solution(mesh):
    nz = mesh.shape["cells"] // 2
    side = {16: 4, 4: 2}[mesh.shape["genes"]]
    nh = nz // 2

    def local(sketch, tiles, tile_rows, tile_cols, tile_counts):
        slots = tiles.shape[0]
        rows, rank = sketch.shape
        part = rows // (side * side)
        dma = pltpu.SemaphoreType.DMA
        kind = jnp.int16 if CODED else F32
        message = (2, PIECES, nh, TILE // PIECES + (SCALE_ROWS if CODED else 0), TILE)
        hbm = pl.BlockSpec(memory_space=pl.ANY)
        vmem = pltpu.VMEM
        return pl.pallas_call(
            functools.partial(kernel, nz, side),
            out_shape=jax.ShapeDtypeStruct((part, rank), F32),
            in_specs=[hbm] * 5,
            out_specs=pl.BlockSpec(memory_space=pltpu.VMEM),
            scratch_shapes=[
                vmem((slots + 1, TILE, TILE), BF16),
                vmem((rows, rank), BF16),
                vmem((1, slots), jnp.int32),
                vmem((1, slots), jnp.int32),
                pltpu.SMEM((1,), jnp.int32),
                vmem((1, rows // TILE * nz), jnp.int32),
                pltpu.SMEM((1, rows // TILE * nz), jnp.int32),
                vmem((rows, nz * TILE), BF16),
                vmem((rank, rows), BF16),
                vmem((nh, rank, TILE), F32),
                vmem((nh, rank, TILE), F32),
                vmem((nh, rank, TILE), F32),
                vmem(message, kind),
                vmem(message, kind),
                vmem((rank, nz * TILE), BF16),
                vmem((PIECES, side, part * side, TILE), BF16),
                vmem((PIECES, part * side, TILE), F32),
                vmem((PIECES, side * side, part, TILE), BF16),
                dma((6,)),
                dma((nh // 2,)),
                dma((nh // 2,)),
                dma((2, PIECES, nh)),
                dma((2, PIECES, nh)),
                dma((2, PIECES, nh)),
                dma((2, PIECES, nh)),
                dma((1 + 2 * nh, PIECES)),
                dma((1 + 2 * nh, PIECES)),
                dma((PIECES, side * side)),
                dma((PIECES, side * side)),
                pltpu.SemaphoreType.REGULAR((3,)),
            ],
            compiler_params=pltpu.CompilerParams(
                collective_id=0, has_side_effects=True, vmem_limit_bytes=67_000_000),
            name="power_pass",
        )(sketch, tiles, tile_rows.reshape(1, -1), tile_cols.reshape(1, -1), tile_counts)

    in_specs = (
        P("cells", None),
        P(("cells", "genes"), None, None),
        P(("cells", "genes")),
        P(("cells", "genes")),
        P(("cells", "genes")),
    )
    return jax.shard_map(
        local, mesh=mesh, in_specs=in_specs, out_specs=P(("cells", "genes"), None), check_vma=False)
```

```python
import functools

import jax
import jax.numpy as jnp
from jax import lax
from jax.experimental import pallas as pl
from jax.experimental.pallas import tpu as pltpu
from jax.sharding import PartitionSpec as P

MESH = pl.DeviceIdType.MESH
TILE = 128
PIECES = 2
CODED = True
PEAK = 32700.0
SCALE_ROWS = 16
ORDER = (2, 1, 3, 0)
UP = {1: 0, 2: 0, 3: 2, 4: 2, 5: 0, 6: 5, 7: 5, 8: 5}
F32 = jnp.float32
BF16 = jnp.bfloat16


def mult(value, of):
    return pl.multiple_of(value, of)


def kernel(
    nz, side, sketch_hbm, tiles_hbm, rows_hbm, cols_hbm, count_hbm, out_ref,
    tiles, sketch, ids_r, ids_c, count, slot_v, slot_s, dense, qt, own, oth, prt,
    first, rr, gath, ysend, yown, yrecv,
    in_sem, prt_send, prt_recv, rs_send, rs_recv, ag_send, ag_recv, pg_send, pg_recv, y_send, y_recv, hint,
):
    slots = tiles_hbm.shape[0]
    rank = sketch_hbm.shape[1]
    nh = nz // 2
    half = nz // 2 * TILE
    blocks = nz
    row_blocks = sketch_hbm.shape[0] // TILE
    pr = TILE // PIECES

    cells = lax.axis_index("cells")
    genes = lax.axis_index("genes")
    z, core = cells // 2, cells % 2
    gx, gy = genes // side, genes % side
    twin = (z * 2 + 1 - core, genes)

    def along(way, n):
        return ((z + n) % nz if way == 0 else (z + nz - n) % nz)

    def ring(way, n):
        return (along(way, n) * 2 + core, genes)

    steps = sorted({j - UP[j] for j in range(1, nh + 1)} & {1, 2, 3})
    reach = sorted({n % nz for d in steps for n in (d, nz - d)})

    def peer(ox, oy):
        return (cells, (gx + ox) % side * side + (gy + oy) % side)

    offsets = [(ox, oy) for ox in range(side) for oy in range(side)][1:]
    close = [(ox, oy) for ox, oy in offsets if min(ox, side - ox) + min(oy, side - oy) <= 2]
    hints = [(1, 0), (side - 1, 0), (1, 1)] if len(close) < len(offsets) else []

    barrier = pltpu.get_barrier_semaphore()
    greeted = [ring(0, n) for n in reach] + [twin] + [peer(ox, oy) for ox, oy in close]
    for who in greeted:
        pl.semaphore_signal(barrier, inc=1, device_id=who, device_id_type=MESH)

    loads = [
        pltpu.make_async_copy(rows_hbm, ids_r, in_sem.at[0]),
        pltpu.make_async_copy(cols_hbm, ids_c, in_sem.at[1]),
        pltpu.make_async_copy(count_hbm, count, in_sem.at[2]),
        pltpu.make_async_copy(sketch_hbm, sketch, in_sem.at[3]),
        pltpu.make_async_copy(tiles_hbm, tiles.at[pl.ds(0, slots)], in_sem.at[4]),
    ]
    for load in loads:
        load.start()

    tiles[slots] = jnp.zeros((TILE, TILE), BF16)
    for load in loads[:3]:
        load.wait()
    lane = lax.broadcasted_iota(jnp.int32, (1, slots), 1)
    key = jnp.where(lane < count[0], ids_r[...] * blocks + ids_c[...], -1)
    total = row_blocks * blocks
    where_j = lax.broadcasted_iota(jnp.int32, (total, slots), 0)
    which_s = lax.broadcasted_iota(jnp.int32, (total, slots), 1)
    hit = where_j == jnp.broadcast_to(key, (total, slots))
    picked = jnp.sum(jnp.where(hit, which_s - slots, 0), axis=1, keepdims=True) + slots
    diag = lax.broadcasted_iota(jnp.int32, (total, total), 0) == lax.broadcasted_iota(jnp.int32, (total, total), 1)
    row = jnp.sum(jnp.where(diag, jnp.broadcast_to(picked, (total, total)), 0), axis=0, keepdims=True)
    slot_v[...] = row
    to_smem = pltpu.make_async_copy(slot_v, slot_s, in_sem.at[5])
    to_smem.start()

    loads[3].wait()
    qt[...] = jnp.transpose(sketch[...])
    to_smem.wait()
    loads[4].wait()

    def place(r, carry):
        at = mult(r * TILE, TILE)
        for c in range(blocks):
            dense[pl.ds(at, TILE), c * TILE:(c + 1) * TILE] = tiles[jnp.clip(slot_s[0, r * blocks + c], 0, slots)]
        return carry
    lax.fori_loop(0, row_blocks, place, 0)

    pairs = nh // 2
    order_q = [(z // 4 + o) % pairs for o in ORDER if o < pairs]

    def product(offset, into):
        value = jnp.dot(qt[...], dense[:, pl.ds(mult(offset, 2 * TILE), 2 * TILE)], preferred_element_type=F32)
        into[0] = value[:, :TILE]
        into[1] = value[:, TILE:]

    for q in order_q:
        product((1 - core) * half + q * 2 * TILE, oth.at[pl.ds(2 * q, 2)])
    for q in order_q:
        product(core * half + q * 2 * TILE, own.at[pl.ds(2 * q, 2)])

    pl.semaphore_wait(barrier, len(greeted))
    for k, (ox, oy) in enumerate(hints):
        pl.semaphore_signal(hint.at[k], inc=1, device_id=peer(side - ox, side - oy), device_id_type=MESH)
    pending = []
    swaps = []
    for k, q in enumerate(order_q):
        swap = pltpu.make_async_remote_copy(
            oth.at[pl.ds(2 * q, 2)], prt.at[pl.ds(2 * q, 2)], prt_send.at[k], prt_recv.at[k],
            device_id=twin, device_id_type=MESH)
        swap.start()
        swaps.append(swap)
        pending.append(swap)
    def mine(d, p):
        at = mult(p * TILE + d % 2 * pr, pr)
        return own[d // 2, pl.ds(at, pr), :] + prt[d // 2, pl.ds(at, pr), :]

    def hops(way, p):
        return nh - (way + p) % 2

    def children(j, n):
        return [c for c in range(1, n + 1) if UP[c] == j]

    def encode(value, into):
        if not CODED:
            into[...] = value
            return
        peak = jnp.max(jnp.abs(value), axis=0, keepdims=True)
        power = jnp.floor(jnp.log2(jnp.maximum(peak, 1e-30))) + 1.0
        into[pl.ds(0, pr)] = jnp.round(value * (jnp.exp2(-power) * PEAK)).astype(jnp.int32).astype(jnp.int16)
        into[pl.ds(pr, SCALE_ROWS)] = jnp.broadcast_to(power, (SCALE_ROWS, TILE)).astype(jnp.int32).astype(jnp.int16)

    def decode(ref):
        if not CODED:
            return ref[...]
        power = ref[pl.ds(pr, SCALE_ROWS)].astype(jnp.int32).astype(F32)[0:1]
        return ref[pl.ds(0, pr)].astype(jnp.int32).astype(F32) * (jnp.exp2(power) * (1.0 / PEAK))

    def rs_copy(way, j, p):
        return pltpu.make_async_remote_copy(
            first.at[way, p, j - 1], rr.at[way, p, j - 1], rs_send.at[way, p, j - 1], rs_recv.at[way, p, j - 1],
            device_id=ring(way, j - UP[j]), device_id_type=MESH)

    def collect(way, j, p, total):
        for c in children(j, hops(way, p)):
            rs_copy(way, c, p).wait_recv()
            total = total + decode(rr.at[way, p, c - 1])
        return total

    deep = [j for j in range(nh, 0, -1) if UP[j]]
    heads = [j for j in range(nh, 0, -1) if not UP[j] and children(j, nh)]
    near = [j for j in range(nh, 0, -1) if not UP[j] and not children(j, nh)]
    def forward(j, p):
        ways = [way for way in range(2) if j <= hops(way, p)]
        for way in ways:
            encode(collect(way, j, p, mine(along(way, j), p)), first.at[way, p, j - 1])
        for way in ways:
            copy = rs_copy(way, j, p)
            copy.start()
            pending.append(copy)

    ready = {deep[0]: swaps[:1], deep[1]: swaps[1:3], deep[-1]: swaps[3:]} if len(swaps) == 4 else {nh: swaps}
    for j in deep or [nh]:
        for swap in ready.get(j, ()):
            swap.wait_recv()
        if j in deep:
            forward(j, 0)
    for p, group in ((1, deep), (0, heads + near), (1, heads + near)):
        for j in group:
            forward(j, p)

    def place_of(who, d, p):
        return gath.at[pl.ds(mult(p * TILE + d % 2 * pr, pr), pr), pl.ds(mult(who * half + d // 2 * TILE, TILE), TILE)]

    def ag_copy(way, j, p, d):
        there = place_of(core, d, p)
        return pltpu.make_async_remote_copy(
            there, there, ag_send.at[way, p, j - 1], ag_recv.at[way, p, j - 1],
            device_id=ring(way, j - UP[j]), device_id_type=MESH)

    def pg_copy(index, p, who, d):
        there = place_of(who, d, p)
        return pltpu.make_async_remote_copy(
            there, there, pg_send.at[index, p], pg_recv.at[index, p], device_id=twin, device_id_type=MESH)

    def spread(way, j, p, d):
        for c in reversed(children(j, hops(way, p))):
            copy = ag_copy(way, c, p, d)
            copy.start()
            pending.append(copy)

    def share(index, p, d):
        copy = pg_copy(index, p, core, d)
        copy.start()
        pending.append(copy)

    def receive(j, p):
        for way in range(2):
            if j > hops(way, p):
                continue
            d = along(1 - way, j)
            ag_copy(way, j, p, d).wait_recv()
            spread(way, j, p, d)
            share(1 + way * nh + j - 1, p, d)

    def receive_shared(p):
        pg_copy(0, p, 1 - core, z).wait_recv()
        for j in range(1, nh + 1):
            for way in range(2):
                if j <= hops(way, p):
                    pg_copy(1 + way * nh + j - 1, p, 1 - core, along(1 - way, j)).wait_recv()

    for p in range(PIECES):
        total = mine(z, p)
        for way in range(2):
            total = collect(way, 0, p, total)
        place_of(core, z, p)[...] = total.astype(BF16)
        for way in range(2):
            spread(way, 0, p, z)
        share(0, p, z)

    part = dense.shape[0] // (side * side)
    wide = part * side
    landings = [[], []]
    order = [side // 2] + [o for o in range(1, side) if o != side // 2] + [0]

    def project(ox, p):
        at = mult((gx + ox) % side * wide, wide)
        value = lax.dot_general(
            dense[pl.ds(at, wide), :], gath[p * TILE:(p + 1) * TILE, :], (((1,), (1,)), ((), ())),
            preferred_element_type=F32)
        if ox == 0:
            yown[p] = value
        ysend[p, ox] = value.astype(BF16)
        for oy in order:
            if ox == 0 and oy == 0:
                continue
            index = ox * side + oy
            copy = pltpu.make_async_remote_copy(
                ysend.at[p, ox, pl.ds(mult((gy + oy) % side * part, part), part)], yrecv.at[p, index],
                y_send.at[p, index], y_recv.at[p, index], device_id=peer(ox, oy), device_id_type=MESH)
            copy.start()
            pending.append(copy)
            landings[p].append((index, copy))

    for k in range(len(hints)):
        pl.semaphore_wait(hint.at[k], 1)
    for p in range(PIECES):
        for j in heads[::-1]:
            receive(j, p)
    for j in near + deep[::-1]:
        receive(j, 0)
    receive_shared(0)
    later = near + deep[::-1]
    taken = (0, 0, 3, 4)
    for k, ox in enumerate(order):
        project(ox, 0)
        for j in later[taken[k]:taken[k + 1] if k + 1 < side else len(later)]:
            receive(j, 1)
    receive_shared(1)
    for ox in order:
        project(ox, 1)
    def finish(p):
        result = yown[p, pl.ds(mult(gy * part, part), part), :]
        for index, copy in landings[p]:
            copy.wait_recv()
            result = result + yrecv[p, index].astype(F32)
        out_ref[:, p * TILE:(p + 1) * TILE] = result

    finish(0)
    for copy in pending:
        copy.wait_send()
    finish(1)


def solution(mesh):
    nz = mesh.shape["cells"] // 2
    side = {16: 4, 4: 2}[mesh.shape["genes"]]
    nh = nz // 2

    def local(sketch, tiles, tile_rows, tile_cols, tile_counts):
        slots = tiles.shape[0]
        rows, rank = sketch.shape
        part = rows // (side * side)
        dma = pltpu.SemaphoreType.DMA
        kind = jnp.int16 if CODED else F32
        message = (2, PIECES, nh, TILE // PIECES + (SCALE_ROWS if CODED else 0), TILE)
        hbm = pl.BlockSpec(memory_space=pl.ANY)
        vmem = pltpu.VMEM
        return pl.pallas_call(
            functools.partial(kernel, nz, side),
            out_shape=jax.ShapeDtypeStruct((part, rank), F32),
            in_specs=[hbm] * 5,
            out_specs=pl.BlockSpec(memory_space=pltpu.VMEM),
            scratch_shapes=[
                vmem((slots + 1, TILE, TILE), BF16),
                vmem((rows, rank), BF16),
                vmem((1, slots), jnp.int32),
                vmem((1, slots), jnp.int32),
                pltpu.SMEM((1,), jnp.int32),
                vmem((1, rows // TILE * nz), jnp.int32),
                pltpu.SMEM((1, rows // TILE * nz), jnp.int32),
                vmem((rows, nz * TILE), BF16),
                vmem((rank, rows), BF16),
                vmem((nh, rank, TILE), F32),
                vmem((nh, rank, TILE), F32),
                vmem((nh, rank, TILE), F32),
                vmem(message, kind),
                vmem(message, kind),
                vmem((rank, nz * TILE), BF16),
                vmem((PIECES, side, part * side, TILE), BF16),
                vmem((PIECES, part * side, TILE), F32),
                vmem((PIECES, side * side, part, TILE), BF16),
                dma((6,)),
                dma((nh // 2,)),
                dma((nh // 2,)),
                dma((2, PIECES, nh)),
                dma((2, PIECES, nh)),
                dma((2, PIECES, nh)),
                dma((2, PIECES, nh)),
                dma((1 + 2 * nh, PIECES)),
                dma((1 + 2 * nh, PIECES)),
                dma((PIECES, side * side)),
                dma((PIECES, side * side)),
                pltpu.SemaphoreType.REGULAR((3,)),
            ],
            compiler_params=pltpu.CompilerParams(
                collective_id=0, has_side_effects=True, vmem_limit_bytes=67_000_000),
            name="power_pass",
        )(sketch, tiles, tile_rows.reshape(1, -1), tile_cols.reshape(1, -1), tile_counts)

    in_specs = (
        P("cells", None),
        P(("cells", "genes"), None, None),
        P(("cells", "genes")),
        P(("cells", "genes")),
        P(("cells", "genes")),
    )
    return jax.shard_map(
        local, mesh=mesh, in_specs=in_specs, out_specs=P(("cells", "genes"), None), check_vma=False)
```

```python
import functools

import jax
import jax.numpy as jnp
from jax import lax
from jax.experimental import pallas as pl
from jax.experimental.pallas import tpu as pltpu
from jax.sharding import PartitionSpec as P

MESH = pl.DeviceIdType.MESH
TILE = 128
PIECES = 2
CODED = True
PEAK = 32700.0
SCALE_ROWS = 8
ORDER = (2, 1, 3, 0)
UP = {1: 0, 2: 0, 3: 2, 4: 2, 5: 0, 6: 5, 7: 5, 8: 5}
F32 = jnp.float32
BF16 = jnp.bfloat16


def mult(value, of):
    return pl.multiple_of(value, of)


def kernel(
    nz, side, sketch_hbm, tiles_hbm, rows_hbm, cols_hbm, count_hbm, out_ref,
    tiles, sketch, ids_r, ids_c, count, slot_v, slot_s, dense, qt, own, oth, prt,
    first, rr, gath, ysend, yown, yrecv,
    in_sem, prt_send, prt_recv, rs_send, rs_recv, ag_send, ag_recv, pg_send, pg_recv, y_send, y_recv, hint,
):
    slots = tiles_hbm.shape[0]
    rank = sketch_hbm.shape[1]
    nh = nz // 2
    half = nz // 2 * TILE
    blocks = nz
    row_blocks = sketch_hbm.shape[0] // TILE
    pr = TILE // PIECES

    cells = lax.axis_index("cells")
    genes = lax.axis_index("genes")
    z, core = cells // 2, cells % 2
    gx, gy = genes // side, genes % side
    twin = (z * 2 + 1 - core, genes)

    def along(way, n):
        return ((z + n) % nz if way == 0 else (z + nz - n) % nz)

    def ring(way, n):
        return (along(way, n) * 2 + core, genes)

    steps = sorted({j - UP[j] for j in range(1, nh + 1)} & {1, 2, 3})
    reach = sorted({n % nz for d in steps for n in (d, nz - d)})

    def peer(ox, oy):
        return (cells, (gx + ox) % side * side + (gy + oy) % side)

    offsets = [(ox, oy) for ox in range(side) for oy in range(side)][1:]
    close = [(ox, oy) for ox, oy in offsets if min(ox, side - ox) + min(oy, side - oy) <= 2]
    hints = [(1, 0), (side - 1, 0), (1, 1)] if len(close) < len(offsets) else []

    barrier = pltpu.get_barrier_semaphore()
    greeted = [ring(0, n) for n in reach] + [twin] + [peer(ox, oy) for ox, oy in close]
    for who in greeted:
        pl.semaphore_signal(barrier, inc=1, device_id=who, device_id_type=MESH)

    loads = [
        pltpu.make_async_copy(rows_hbm, ids_r, in_sem.at[0]),
        pltpu.make_async_copy(cols_hbm, ids_c, in_sem.at[1]),
        pltpu.make_async_copy(count_hbm, count, in_sem.at[2]),
        pltpu.make_async_copy(sketch_hbm, sketch, in_sem.at[3]),
        pltpu.make_async_copy(tiles_hbm, tiles.at[pl.ds(0, slots)], in_sem.at[4]),
    ]
    for load in loads:
        load.start()

    tiles[slots] = jnp.zeros((TILE, TILE), BF16)
    for load in loads[:3]:
        load.wait()
    lane = lax.broadcasted_iota(jnp.int32, (1, slots), 1)
    key = jnp.where(lane < count[0], ids_r[...] * blocks + ids_c[...], -1)
    total = row_blocks * blocks
    where_j = lax.broadcasted_iota(jnp.int32, (total, slots), 0)
    which_s = lax.broadcasted_iota(jnp.int32, (total, slots), 1)
    hit = where_j == jnp.broadcast_to(key, (total, slots))
    picked = jnp.sum(jnp.where(hit, which_s - slots, 0), axis=1, keepdims=True) + slots
    diag = lax.broadcasted_iota(jnp.int32, (total, total), 0) == lax.broadcasted_iota(jnp.int32, (total, total), 1)
    row = jnp.sum(jnp.where(diag, jnp.broadcast_to(picked, (total, total)), 0), axis=0, keepdims=True)
    slot_v[...] = row
    to_smem = pltpu.make_async_copy(slot_v, slot_s, in_sem.at[5])
    to_smem.start()

    loads[3].wait()
    qt[...] = jnp.transpose(sketch[...])
    to_smem.wait()
    loads[4].wait()

    def place(r, carry):
        at = mult(r * TILE, TILE)
        for c in range(blocks):
            dense[pl.ds(at, TILE), c * TILE:(c + 1) * TILE] = tiles[jnp.clip(slot_s[0, r * blocks + c], 0, slots)]
        return carry
    lax.fori_loop(0, row_blocks, place, 0)

    pairs = nh // 2
    order_q = [(z // 4 + o) % pairs for o in ORDER if o < pairs]

    def product(offset, into):
        value = jnp.dot(qt[...], dense[:, pl.ds(mult(offset, 2 * TILE), 2 * TILE)], preferred_element_type=F32)
        into[0] = value[:, :TILE]
        into[1] = value[:, TILE:]

    for q in order_q:
        product((1 - core) * half + q * 2 * TILE, oth.at[pl.ds(2 * q, 2)])
    for q in order_q:
        product(core * half + q * 2 * TILE, own.at[pl.ds(2 * q, 2)])

    pl.semaphore_wait(barrier, len(greeted))
    for k, (ox, oy) in enumerate(hints):
        pl.semaphore_signal(hint.at[k], inc=1, device_id=peer(side - ox, side - oy), device_id_type=MESH)
    pending = []
    swaps = []
    for k, q in enumerate(order_q):
        swap = pltpu.make_async_remote_copy(
            oth.at[pl.ds(2 * q, 2)], prt.at[pl.ds(2 * q, 2)], prt_send.at[k], prt_recv.at[k],
            device_id=twin, device_id_type=MESH)
        swap.start()
        swaps.append(swap)
        pending.append(swap)
    def mine(d, p):
        at = mult(p * TILE + d % 2 * pr, pr)
        return own[d // 2, pl.ds(at, pr), :] + prt[d // 2, pl.ds(at, pr), :]

    def hops(way, p):
        return nh - (way + p) % 2

    def children(j, n):
        return [c for c in range(1, n + 1) if UP[c] == j]

    def encode(value, into):
        if not CODED:
            into[...] = value
            return
        peak = jnp.max(jnp.abs(value), axis=0, keepdims=True)
        power = jnp.floor(jnp.log2(jnp.maximum(peak, 1e-30))) + 1.0
        into[pl.ds(0, pr)] = jnp.round(value * (jnp.exp2(-power) * PEAK)).astype(jnp.int32).astype(jnp.int16)
        into[pl.ds(pr, SCALE_ROWS)] = jnp.broadcast_to(power, (SCALE_ROWS, TILE)).astype(jnp.int32).astype(jnp.int16)

    def decode(ref):
        if not CODED:
            return ref[...]
        power = ref[pl.ds(pr, SCALE_ROWS)].astype(jnp.int32).astype(F32)[0:1]
        return ref[pl.ds(0, pr)].astype(jnp.int32).astype(F32) * (jnp.exp2(power) * (1.0 / PEAK))

    def rs_copy(way, j, p):
        return pltpu.make_async_remote_copy(
            first.at[way, p, j - 1], rr.at[way, p, j - 1], rs_send.at[way, p, j - 1], rs_recv.at[way, p, j - 1],
            device_id=ring(way, j - UP[j]), device_id_type=MESH)

    def collect(way, j, p, total):
        for c in children(j, hops(way, p)):
            rs_copy(way, c, p).wait_recv()
            total = total + decode(rr.at[way, p, c - 1])
        return total

    deep = [j for j in range(nh, 0, -1) if UP[j]]
    heads = [j for j in range(nh, 0, -1) if not UP[j] and children(j, nh)]
    near = [j for j in range(nh, 0, -1) if not UP[j] and not children(j, nh)]
    def forward(j, p):
        ways = [way for way in range(2) if j <= hops(way, p)]
        for way in ways:
            encode(collect(way, j, p, mine(along(way, j), p)), first.at[way, p, j - 1])
        for way in ways:
            copy = rs_copy(way, j, p)
            copy.start()
            pending.append(copy)

    ready = {deep[0]: swaps[:1], deep[1]: swaps[1:3], deep[-1]: swaps[3:]} if len(swaps) == 4 else {nh: swaps}
    for j in deep or [nh]:
        for swap in ready.get(j, ()):
            swap.wait_recv()
        if j in deep:
            forward(j, 0)
    for p, group in ((1, deep), (0, heads + near), (1, heads + near)):
        for j in group:
            forward(j, p)

    def place_of(who, d, p):
        return gath.at[pl.ds(mult(p * TILE + d % 2 * pr, pr), pr), pl.ds(mult(who * half + d // 2 * TILE, TILE), TILE)]

    def ag_copy(way, j, p, d):
        there = place_of(core, d, p)
        return pltpu.make_async_remote_copy(
            there, there, ag_send.at[way, p, j - 1], ag_recv.at[way, p, j - 1],
            device_id=ring(way, j - UP[j]), device_id_type=MESH)

    def pg_copy(index, p, who, d):
        there = place_of(who, d, p)
        return pltpu.make_async_remote_copy(
            there, there, pg_send.at[index, p], pg_recv.at[index, p], device_id=twin, device_id_type=MESH)

    def spread(way, j, p, d):
        for c in reversed(children(j, hops(way, p))):
            copy = ag_copy(way, c, p, d)
            copy.start()
            pending.append(copy)

    def share(index, p, d):
        copy = pg_copy(index, p, core, d)
        copy.start()
        pending.append(copy)

    def receive(j, p):
        for way in range(2):
            if j > hops(way, p):
                continue
            d = along(1 - way, j)
            ag_copy(way, j, p, d).wait_recv()
            spread(way, j, p, d)
            share(1 + way * nh + j - 1, p, d)

    def receive_shared(p):
        pg_copy(0, p, 1 - core, z).wait_recv()
        for j in range(1, nh + 1):
            for way in range(2):
                if j <= hops(way, p):
                    pg_copy(1 + way * nh + j - 1, p, 1 - core, along(1 - way, j)).wait_recv()

    for p in range(PIECES):
        total = mine(z, p)
        for way in range(2):
            total = collect(way, 0, p, total)
        place_of(core, z, p)[...] = total.astype(BF16)
        for way in range(2):
            spread(way, 0, p, z)
        share(0, p, z)

    part = dense.shape[0] // (side * side)
    wide = part * side
    landings = [[], []]
    order = [side // 2] + [o for o in range(1, side) if o != side // 2] + [0]

    def project(ox, p):
        at = mult((gx + ox) % side * wide, wide)
        value = lax.dot_general(
            dense[pl.ds(at, wide), :], gath[p * TILE:(p + 1) * TILE, :], (((1,), (1,)), ((), ())),
            preferred_element_type=F32)
        if ox == 0:
            yown[p] = value
        ysend[p, ox] = value.astype(BF16)
        for oy in order:
            if ox == 0 and oy == 0:
                continue
            index = ox * side + oy
            copy = pltpu.make_async_remote_copy(
                ysend.at[p, ox, pl.ds(mult((gy + oy) % side * part, part), part)], yrecv.at[p, index],
                y_send.at[p, index], y_recv.at[p, index], device_id=peer(ox, oy), device_id_type=MESH)
            copy.start()
            pending.append(copy)
            landings[p].append((index, copy))

    for k in range(len(hints)):
        pl.semaphore_wait(hint.at[k], 1)
    for p in range(PIECES):
        for j in heads[::-1]:
            receive(j, p)
    for j in near + deep[::-1]:
        receive(j, 0)
    receive_shared(0)
    later = near + deep[::-1]
    taken = (0, 0, 3, 4)
    for k, ox in enumerate(order):
        project(ox, 0)
        for j in later[taken[k]:taken[k + 1] if k + 1 < side else len(later)]:
            receive(j, 1)
    receive_shared(1)
    for ox in order:
        project(ox, 1)
    def finish(p):
        result = yown[p, pl.ds(mult(gy * part, part), part), :]
        for index, copy in landings[p]:
            copy.wait_recv()
            result = result + yrecv[p, index].astype(F32)
        out_ref[:, p * TILE:(p + 1) * TILE] = result

    finish(0)
    for copy in pending:
        copy.wait_send()
    finish(1)


def solution(mesh):
    nz = mesh.shape["cells"] // 2
    side = {16: 4, 4: 2}[mesh.shape["genes"]]
    nh = nz // 2

    def local(sketch, tiles, tile_rows, tile_cols, tile_counts):
        slots = tiles.shape[0]
        rows, rank = sketch.shape
        part = rows // (side * side)
        dma = pltpu.SemaphoreType.DMA
        kind = jnp.int16 if CODED else F32
        message = (2, PIECES, nh, TILE // PIECES + (SCALE_ROWS if CODED else 0), TILE)
        hbm = pl.BlockSpec(memory_space=pl.ANY)
        vmem = pltpu.VMEM
        return pl.pallas_call(
            functools.partial(kernel, nz, side),
            out_shape=jax.ShapeDtypeStruct((part, rank), F32),
            in_specs=[hbm] * 5,
            out_specs=pl.BlockSpec(memory_space=pltpu.VMEM),
            scratch_shapes=[
                vmem((slots + 1, TILE, TILE), BF16),
                vmem((rows, rank), BF16),
                vmem((1, slots), jnp.int32),
                vmem((1, slots), jnp.int32),
                pltpu.SMEM((1,), jnp.int32),
                vmem((1, rows // TILE * nz), jnp.int32),
                pltpu.SMEM((1, rows // TILE * nz), jnp.int32),
                vmem((rows, nz * TILE), BF16),
                vmem((rank, rows), BF16),
                vmem((nh, rank, TILE), F32),
                vmem((nh, rank, TILE), F32),
                vmem((nh, rank, TILE), F32),
                vmem(message, kind),
                vmem(message, kind),
                vmem((rank, nz * TILE), BF16),
                vmem((PIECES, side, part * side, TILE), BF16),
                vmem((PIECES, part * side, TILE), F32),
                vmem((PIECES, side * side, part, TILE), BF16),
                dma((6,)),
                dma((nh // 2,)),
                dma((nh // 2,)),
                dma((2, PIECES, nh)),
                dma((2, PIECES, nh)),
                dma((2, PIECES, nh)),
                dma((2, PIECES, nh)),
                dma((1 + 2 * nh, PIECES)),
                dma((1 + 2 * nh, PIECES)),
                dma((PIECES, side * side)),
                dma((PIECES, side * side)),
                pltpu.SemaphoreType.REGULAR((3,)),
            ],
            compiler_params=pltpu.CompilerParams(
                collective_id=0, has_side_effects=True, vmem_limit_bytes=67_000_000),
            name="power_pass",
        )(sketch, tiles, tile_rows.reshape(1, -1), tile_cols.reshape(1, -1), tile_counts)

    in_specs = (
        P("cells", None),
        P(("cells", "genes"), None, None),
        P(("cells", "genes")),
        P(("cells", "genes")),
        P(("cells", "genes")),
    )
    return jax.shard_map(
        local, mesh=mesh, in_specs=in_specs, out_specs=P(("cells", "genes"), None), check_vma=False)
```
